256 devices in a mesh: slab: 64 (over y, z, core), layer: 4 (over x).
Axes of the slice: x: 4, y: 4, z: 8, core: 2. Of those that a mesh axis runs over, the one named last changes fastest.
Arguments:
- hamilton_blocks: bfloat16 [1024, 128, 128], P(('slab', 'layer')), may hold values from -0.25 to 0.25
- pair_ids: int32 [256, 10], P(('slab', 'layer')), may hold values from 0 to 1023, as said below
- weights: float32 [256, 10], P(('slab', 'layer')), may hold values from 0.25 to 4
- potential: float32 [1], replicated, may hold values from -1 to 1
Outputs:
- density: float32 [1024, 128, 128], P(('slab', 'layer'))
- energy: float32 [1024, 128, 128], P(('slab', 'layer'))
The draws below stay inside these ranges and needn't reach their ends.
Inputs may be any that keep to these rules, and one draw needn't show every extreme that they name: `pair_ids`: the entries of one row are distinct. Slot p is owned by device p // 4, whose slab index is that device // 4 and layer index that device % 4. Row d names only slots owned by devices whose slab index is that of device d, or one more or one less cyclically over 64, with any layer index. A row names at most 4 slots of any one device, and exactly 4 of some device; in every draw some device has exactly 4 of its slots named by each of the 3 * 4 rows that may name its slots.
All inputs are finite; a program needn't handle non-finite values.
Results may differ from the reference program's by a relative error of at most 0.0017.
Values may be sent and summed in bfloat16 or wider, within the bound.
A program may use at most 64 MiB of HBM per device.

```python
import math
import jax
import jax.numpy as jnp
import numpy as np
from jax import lax

BS = 128
NB = 4
PAIRS_DEV = 4
CAP = 4
ITERS = 2
NPS = 10
ORDER = 512
NPAIRS = 1024
N_SLAB = 64
N_LAYER = 4
DEVICES = 256


def draw_pair_ids(key, part):
    owners = 3 * N_LAYER
    base = jax.random.fold_in(key, 17)
    shift_key = jax.random.fold_in(base, 1)
    layer_key = jax.random.fold_in(base, 2)
    pool_key = jax.random.fold_in(base, 3)
    slot_key = jax.random.fold_in(base, 4)
    order_key = jax.random.fold_in(base, 5)
    residue = jax.random.randint(shift_key, (), 0, 3)
    hub_layers = jax.random.randint(layer_key, (N_SLAB,), 0, N_LAYER)
    device = jnp.arange(DEVICES, dtype=jnp.int32)
    here_slab = device // N_LAYER
    offsets = jnp.arange(3, dtype=jnp.int32)
    near_slab = (here_slab[:, None] + offsets[None, :] - 1 + N_SLAB) % N_SLAB
    marked = near_slab % 3 == residue
    first_mark = jnp.min(jnp.where(marked, offsets[None, :], 3), axis=1)
    hub_offset = jnp.where(first_mark == 3, 1, first_mark)
    hub_slab = (here_slab + hub_offset - 1 + N_SLAB) % N_SLAB
    hub_local = (hub_offset * N_LAYER + hub_layers[hub_slab]).astype(jnp.int32)
    pool_base = jnp.repeat(jnp.arange(owners - 1, dtype=jnp.int32), CAP)

    def pick_rest(subkey):
        return jax.random.permutation(subkey, pool_base)[:NPS - CAP]
    rest = jax.vmap(pick_rest)(jax.random.split(pool_key, DEVICES)).astype(jnp.int32)
    rest = rest + (rest >= hub_local[:, None]).astype(jnp.int32)
    labels = jnp.concatenate([jnp.broadcast_to(hub_local[:, None], (DEVICES, CAP)), rest], axis=1)
    items = jnp.arange(NPS, dtype=jnp.int32)
    same = labels[:, :, None] == labels[:, None, :]
    earlier = items[None, :] < items[:, None]
    ranks = jnp.sum(jnp.logical_and(same, earlier[None]), axis=2).astype(jnp.int32)

    def slot_order(subkey):
        return jax.random.permutation(subkey, PAIRS_DEV)
    slot_perms = jax.vmap(slot_order)(jax.random.split(slot_key, DEVICES * owners)).astype(jnp.int32)
    slot_perms = slot_perms.reshape(DEVICES, owners, PAIRS_DEV)
    slots = slot_perms[device[:, None], labels, ranks]

    def item_order(subkey):
        return jax.random.permutation(subkey, NPS)
    orders = jax.vmap(item_order)(jax.random.split(order_key, DEVICES)).astype(jnp.int32)
    labels = jnp.take_along_axis(labels, orders, axis=1)
    slots = jnp.take_along_axis(slots, orders, axis=1)
    owner_slab = (here_slab[:, None] + labels // N_LAYER - 1 + N_SLAB) % N_SLAB
    owner_layer = labels % N_LAYER
    return ((owner_slab * N_LAYER + owner_layer) * PAIRS_DEV + slots).astype(jnp.int32)


def shard_levels(stream_key, extent, pieces, smallest, top_value):
    level = 1.0
    for dim, blocks in pieces:
        heights = jax.random.uniform(jax.random.fold_in(jax.random.fold_in(stream_key, 6), dim), (blocks,), jnp.float32, smallest / len(pieces), top_value / len(pieces))
        level = level * jnp.repeat(jnp.exp(heights), extent[dim] // blocks).reshape((-1,) + (1,) * (len(extent) - 1 - dim))
    return level


def noise(key, shape, scale, reach, cuts=(), held_as=jnp.bfloat16):
    values = jax.random.normal(key, shape, jnp.float32) * scale
    if len(cuts) > 0:
        values = shard_levels(key, shape, cuts, -0.22, 0.18) * values
    return jnp.clip(values, min=-reach, max=reach).astype(held_as)


def setup_inputs(seed: int = 0) -> dict:
    keys = jax.random.split(jax.random.key(seed), 5)
    return {
        "hamilton_blocks": noise(keys[0], (NPAIRS, BS, BS), ORDER ** -0.5, 0.25, ((0, 256),)),
        "pair_ids": draw_pair_ids(jax.random.fold_in(keys[4], 71), 0),
        "weights": jnp.clip(jnp.exp(math.log(4.0) - 2.7725887 * jax.random.uniform(keys[2], (DEVICES, NPS), jnp.float32) ** shard_levels(keys[2], (DEVICES, NPS), ((0, 256),), -0.2, 0.2)), 0.25, 4.0),
        "potential": jnp.clip(jax.random.uniform(keys[3], (1,), jnp.float32, -1.0, 1.0), -1.0, 1.0),
    }


def submatrix_step(blocks, weight_row, mu_value):
    block_rows, block_cols = np.triu_indices(NB)
    block_rows = block_rows.astype(np.int32)
    block_cols = block_cols.astype(np.int32)
    upper_grid = jnp.zeros((NB, NB, BS, BS), jnp.float32).at[block_rows, block_cols].set(blocks.astype(jnp.float32))
    sub_order = NB * BS
    upper = upper_grid.transpose(0, 2, 1, 3).reshape(sub_order, sub_order)
    hamilt = upper + upper.T
    identity = jnp.eye(sub_order, dtype=jnp.float32)
    shifted = mu_value * identity - hamilt
    norm_scale = 2.0 * jnp.sqrt(jnp.sum(shifted * shifted) / sub_order + 1e-06)
    iterate = shifted / norm_scale
    for iteration in range(ITERS):
        square = jnp.dot(iterate, iterate, precision=lax.Precision.HIGHEST, preferred_element_type=jnp.float32)
        iterate = 1.5 * iterate - 0.5 * jnp.dot(iterate, square, precision=lax.Precision.HIGHEST, preferred_element_type=jnp.float32)
    dens_sub = 0.5 * (identity + iterate)
    energy_sub = jnp.dot(dens_sub, hamilt, precision=lax.Precision.HIGHEST, preferred_element_type=jnp.float32)
    dens_pairs = dens_sub.reshape(NB, BS, NB, BS).transpose(0, 2, 1, 3)[block_rows, block_cols]
    energy_pairs = energy_sub.reshape(NB, BS, NB, BS).transpose(0, 2, 1, 3)[block_rows, block_cols]
    scaled = weight_row[:, None, None]
    return ((scaled * dens_pairs).astype(jnp.bfloat16), (scaled * energy_pairs).astype(jnp.bfloat16))

def reference(hamilton_blocks, pair_ids, weights, potential):

    def one_device(totals, device):
        requests = pair_ids[device].astype(jnp.int32)
        blocks = hamilton_blocks[requests]
        dens_parts, energy_parts = submatrix_step(blocks, weights[device], potential[0])
        dens_total = totals[0].at[requests].add(dens_parts.astype(jnp.float32))
        energy_total = totals[1].at[requests].add(energy_parts.astype(jnp.float32))
        return ((dens_total, energy_total), None)
    empty = jnp.zeros((NPAIRS, BS, BS), jnp.float32)
    totals, unused = lax.scan(one_device, (empty, empty), jnp.arange(DEVICES, dtype=jnp.int32))
    return (totals[0], totals[1])
```

```python
import functools

import jax
import jax.numpy as jnp
import numpy as np
from jax import lax
from jax.experimental import pallas as pl
from jax.experimental.pallas import tpu as pltpu
from jax.sharding import PartitionSpec as P

BS = 128
NB = 4
NPS = 10
ORDER = 512
SLOTS = 4
MESH = pl.DeviceIdType.MESH
F32 = jnp.float32
BF16 = jnp.bfloat16
PAIRS = [(a, b) for a in range(NB) for b in range(a, NB)]
NO_PART = NPS


def mm(a, b):
    return jnp.dot(a, b, preferred_element_type=F32)


def eye(order, value):
    r = lax.broadcasted_iota(jnp.int32, (order, order), 0)
    c = lax.broadcasted_iota(jnp.int32, (order, order), 1)
    return jnp.where(r == c, value, 0.0)


def mean_diagonal(m):
    total = None
    for a in range(NB):
        s = slice(a * BS, (a + 1) * BS)
        r = lax.broadcasted_iota(jnp.int32, (BS, BS), 0)
        c = lax.broadcasted_iota(jnp.int32, (BS, BS), 1)
        part = jnp.where(r == c, m[s, s], 0.0)
        total = part if total is None else total + part
    return jnp.sum(total, keepdims=True) * (1.0 / ORDER)


def kernel(
    n_slab,
    hb_ref,
    ids_ref,
    w_ref,
    mu_ref,
    dens_ref,
    energy_ref,
    near,
    d_parts,
    e_parts,
    remote_ids,
    inverse,
    h_mat,
    d_sums,
    e_sums,
    d_far,
    e_far,
    d_got,
    e_got,
    local_sem,
    gather_send,
    gather_recv,
    ids_send,
    ids_recv,
    part_send,
    part_recv,
    sum_send,
    sum_recv,
):
    slab = lax.axis_index("slab")
    layer = lax.axis_index("layer")
    core = lax.rem(slab, 2)
    partner_slab = slab + 1 - 2 * core
    other_slab = lax.rem(slab - 1 + 2 * core + n_slab, n_slab)
    up_layer = lax.rem(layer + 1, 4)
    down_layer = lax.rem(layer + 3, 4)
    far_layer = lax.rem(layer + 2, 4)
    up, down = (slab, up_layer), (slab, down_layer)
    partner, other = (partner_slab, layer), (other_slab, layer)

    def remote(src, dst, send, recv, device):
        return pltpu.make_async_remote_copy(
            src_ref=src, dst_ref=dst, send_sem=send, recv_sem=recv, device_id=device, device_id_type=MESH
        )

    own_copy = pltpu.make_async_copy(hb_ref, near.at[pl.ds(layer * SLOTS, SLOTS)], local_sem)
    own_copy.start()

    barrier = pltpu.get_barrier_semaphore()
    for device in (up, down, partner, other):
        pl.semaphore_signal(barrier, inc=1, device_id=device, device_id_type=MESH)
    pl.semaphore_wait(barrier, 4)

    def piece(group, which_layer, first, count):
        return near.at[pl.ds(group * 16 + which_layer * SLOTS + first, count)]

    ids_copies = []
    for j, device in enumerate((partner, other)):
        ids_copies.append(remote(ids_ref, remote_ids.at[j], ids_send.at[j], ids_recv.at[j], device))
        ids_copies[-1].start()

    started = []

    def send(src, group, which_layer, first, count, index, device):
        c = remote(src, piece(group, which_layer, first, count), gather_send.at[index], gather_recv.at[index], device)
        c.start()
        started.append(c)

    send(hb_ref, 2, layer, 0, 4, 0, other)
    send(hb_ref, 0, layer, 0, 4, 1, up)
    send(hb_ref, 0, layer, 0, 4, 2, down)
    send(hb_ref, 1, layer, 0, 4, 3, partner)

    def wait_recv(group, which_layer, first, count, index):
        at = piece(group, which_layer, first, count)
        remote(at, at, gather_send.at[index], gather_recv.at[index], up).wait_recv()

    wait_recv(0, down_layer, 0, 4, 1)
    send(piece(0, down_layer, 0, 2), 0, down_layer, 0, 2, 4, up)
    send(piece(0, down_layer, 0, 4), 2, down_layer, 0, 4, 5, other)
    send(piece(0, down_layer, 0, 4), 1, down_layer, 0, 4, 6, partner)
    wait_recv(0, up_layer, 0, 4, 2)
    send(piece(0, up_layer, 2, 2), 0, up_layer, 2, 2, 7, down)
    send(piece(0, up_layer, 0, 4), 2, up_layer, 0, 4, 8, other)
    send(piece(0, up_layer, 0, 4), 1, up_layer, 0, 4, 9, partner)
    wait_recv(0, far_layer, 0, 2, 4)
    send(piece(0, far_layer, 0, 2), 2, far_layer, 0, 2, 10, other)
    send(piece(0, far_layer, 0, 2), 1, far_layer, 0, 2, 11, partner)
    wait_recv(0, far_layer, 2, 2, 7)
    send(piece(0, far_layer, 2, 2), 2, far_layer, 2, 2, 12, other)
    send(piece(0, far_layer, 2, 2), 1, far_layer, 2, 2, 13, partner)

    zero_block = jnp.zeros((BS, BS), BF16)
    for j in range(3):
        d_parts[j, NO_PART] = zero_block
        e_parts[j, NO_PART] = zero_block
    for c in ids_copies:
        c.wait_recv()

    def find(s, _):
        want = slab * 16 + s
        found = [NO_PART + 0 * want for _ in range(3)]
        for k in range(NPS):
            found[0] = jnp.where(ids_ref[0, k] == want, k, found[0])
            found[1] = jnp.where(remote_ids[0, 0, k] == want, k, found[1])
            found[2] = jnp.where(remote_ids[1, 0, k] == want, k, found[2])
        for j in range(3):
            inverse[j, s] = found[j]
        return 0

    lax.fori_loop(0, 16, find, 0)

    own_copy.wait()
    wait_recv(2, layer, 0, 4, 0)
    wait_recv(1, layer, 0, 4, 3)
    wait_recv(2, down_layer, 0, 4, 5)
    wait_recv(1, down_layer, 0, 4, 6)
    wait_recv(2, up_layer, 0, 4, 8)
    wait_recv(1, up_layer, 0, 4, 9)
    wait_recv(2, far_layer, 0, 2, 10)
    wait_recv(1, far_layer, 0, 2, 11)
    wait_recv(2, far_layer, 2, 2, 12)
    wait_recv(1, far_layer, 2, 2, 13)

    for k, (a, b) in enumerate(PAIRS):
        request = ids_ref[0, k]
        its_slab = request // 16
        group = jnp.where(its_slab == slab, 0, jnp.where(its_slab == partner_slab, 1, 2))
        block = near[group * 16 + request - its_slab * 16].astype(F32)
        ra, rb = pl.ds(a * BS, BS), pl.ds(b * BS, BS)
        if a == b:
            h_mat[ra, ra] = block + block.T
        else:
            h_mat[ra, rb] = block
            h_mat[rb, ra] = block.T
    h = h_mat[...]
    mu = mu_ref[0]
    norm2 = jnp.zeros((BS, BS), F32)
    for a in range(NB):
        for b in range(NB):
            block = h[a * BS : (a + 1) * BS, b * BS : (b + 1) * BS]
            if a == b:
                block = eye(BS, mu) - block
            norm2 += block * block
    norm2 = jnp.sum(norm2, keepdims=True) * (1.0 / ORDER) + 1e-06
    inv = 0.5 * lax.rsqrt(norm2)
    hb = h.astype(BF16)
    x0 = mu * inv
    s0 = (inv * inv) * mm(hb, hb) - (2.0 * x0 * inv) * h + eye(ORDER, x0 * x0 - 0.25)
    x1 = (-1.375 * inv) * h - (0.5 * x0) * s0 + (0.5 * inv) * mm(hb, s0.astype(BF16)) + eye(ORDER, 1.375 * x0)
    t1 = mean_diagonal(x1)
    b1 = x1 - eye(ORDER, t1)
    b1h = b1.astype(BF16)
    s1 = mm(b1h, b1h) + (2.0 * t1) * b1 + eye(ORDER, t1 * t1)
    u1 = mean_diagonal(s1)
    s1 = s1 - eye(ORDER, u1)
    x2 = (1.5 - 0.5 * u1) * x1 - (0.5 * t1) * s1 - 0.5 * mm(b1h, s1.astype(BF16))

    weights = [w_ref[0, k] for k in range(NPS)]
    for k, (a, b) in enumerate(PAIRS):
        block = x2[a * BS : (a + 1) * BS, b * BS : (b + 1) * BS]
        if a == b:
            block = block + eye(BS, 1.0)
        d_parts[0, k] = ((0.5 * weights[k]) * block).astype(BF16)

    part_copies = []

    def send_parts(parts, index):
        for j, device in ((2, other), (1, partner)):
            c = remote(
                parts.at[0, pl.ds(0, NPS)],
                parts.at[j, pl.ds(0, NPS)],
                part_send.at[index + j - 1],
                part_recv.at[index + j - 1],
                device,
            )
            c.start()
            part_copies.append(c)

    send_parts(d_parts, 0)

    t2 = mean_diagonal(x2)
    c2 = x2 - eye(ORDER, t2)
    c2h = c2.astype(BF16)
    c2l = (c2 - c2h.astype(F32)).astype(BF16)
    hl = (h - hb.astype(F32)).astype(BF16)
    e2 = (1.0 + t2) * h + mm(c2h, hb) + mm(c2l, hb) + mm(c2h, hl)
    for k, (a, b) in enumerate(PAIRS):
        block = e2[a * BS : (a + 1) * BS, b * BS : (b + 1) * BS]
        e_parts[0, k] = ((0.5 * weights[k]) * block).astype(BF16)
    send_parts(e_parts, 2)

    def collect(parts, which_layer, j):
        s = which_layer * SLOTS + j
        return (
            parts[0, inverse[0, s]].astype(F32)
            + parts[1, inverse[1, s]].astype(F32)
            + parts[2, inverse[2, s]].astype(F32)
        )

    sum_copies = []

    def total(parts, sums, far, got, out, base):
        part_copies[base // 3].wait_recv()
        part_copies[base // 3 + 1].wait_recv()

        def move(src, dst, index, device):
            c = remote(src, dst, sum_send.at[base + index], sum_recv.at[base + index], device)
            c.start()
            sum_copies.append(c)
            return c

        for j in range(2):
            sums[2, j] = collect(parts, far_layer, j).astype(BF16)
        f_up = move(sums.at[2, pl.ds(0, 2)], far.at[0], 0, up)
        for j in range(2, 4):
            sums[2, j] = collect(parts, far_layer, j).astype(BF16)
        f_down = move(sums.at[2, pl.ds(2, 2)], far.at[1], 1, down)
        for j in range(2, 4):
            sums[0, j] = collect(parts, up_layer, j).astype(BF16)
        h_up = move(sums.at[0, pl.ds(2, 2)], got.at[0, pl.ds(2, 2)], 2, up)
        for j in range(2):
            sums[1, j] = collect(parts, down_layer, j).astype(BF16)
        h_down = move(sums.at[1, pl.ds(0, 2)], got.at[1, pl.ds(0, 2)], 3, down)
        f_up.wait_recv()
        for j in range(2):
            sums[0, j] = (collect(parts, up_layer, j) + far[0, j].astype(F32)).astype(BF16)
        a_up = move(sums.at[0, pl.ds(0, 2)], got.at[0, pl.ds(0, 2)], 4, up)
        f_down.wait_recv()
        for j in range(2, 4):
            sums[1, j] = (collect(parts, down_layer, j) + far[1, j - 2].astype(F32)).astype(BF16)
        a_down = move(sums.at[1, pl.ds(2, 2)], got.at[1, pl.ds(2, 2)], 5, down)
        for j in range(4):
            out[j] = collect(parts, layer, j)
        return h_up, h_down, a_up, a_down

    def finish(waits, got, out):
        for c in waits:
            c.wait_recv()
        for j in range(4):
            out[j] = out[j] + (got[0, j].astype(F32) + got[1, j].astype(F32))

    d_waits = total(d_parts, d_sums, d_far, d_got, dens_ref, 0)
    e_waits = total(e_parts, e_sums, e_far, e_got, energy_ref, 6)
    finish(d_waits, d_got, dens_ref)
    finish(e_waits, e_got, energy_ref)

    for c in ids_copies + started + part_copies + sum_copies:
        c.wait_send()


def solution(mesh):
    n_slab = mesh.shape["slab"]

    def step(hamilton_blocks, pair_ids, weights, potential):
        smem = pl.BlockSpec(memory_space=pltpu.SMEM)
        vmem = pl.BlockSpec(memory_space=pltpu.VMEM)
        dma = pltpu.SemaphoreType.DMA
        out = jax.ShapeDtypeStruct((SLOTS, BS, BS), F32)
        return pl.pallas_call(
            functools.partial(kernel, n_slab),
            out_shape=(out, out),
            in_specs=[pl.BlockSpec(memory_space=pl.ANY), smem, smem, smem],
            out_specs=(vmem, vmem),
            scratch_shapes=[
                pltpu.VMEM((48, BS, BS), BF16),
                pltpu.VMEM((3, NPS + 1, BS, BS), BF16),
                pltpu.VMEM((3, NPS + 1, BS, BS), BF16),
                pltpu.SMEM((2, 1, NPS), jnp.int32),
                pltpu.SMEM((3, 16), jnp.int32),
                pltpu.VMEM((ORDER, ORDER), F32),
                pltpu.VMEM((3, SLOTS, BS, BS), BF16),
                pltpu.VMEM((3, SLOTS, BS, BS), BF16),
                pltpu.VMEM((2, 2, BS, BS), BF16),
                pltpu.VMEM((2, 2, BS, BS), BF16),
                pltpu.VMEM((2, SLOTS, BS, BS), BF16),
                pltpu.VMEM((2, SLOTS, BS, BS), BF16),
                dma,
                dma((14,)),
                dma((14,)),
                dma((2,)),
                dma((2,)),
                dma((4,)),
                dma((4,)),
                dma((12,)),
                dma((12,)),
            ],
            compiler_params=pltpu.CompilerParams(
                collective_id=0, has_side_effects=True, vmem_limit_bytes=48 * 1024 * 1024
            ),
        )(hamilton_blocks, pair_ids, weights, potential)

    return jax.shard_map(
        step,
        mesh=mesh,
        in_specs=(P(("slab", "layer"), None, None), P(("slab", "layer"), None), P(("slab", "layer"), None), P()),
        out_specs=(P(("slab", "layer"), None, None), P(("slab", "layer"), None, None)),
        check_vma=False,
    )
```

```python
import functools

import jax
import jax.numpy as jnp
import numpy as np
from jax import lax
from jax.experimental import pallas as pl
from jax.experimental.pallas import tpu as pltpu
from jax.sharding import PartitionSpec as P

BS = 128
NB = 4
NPS = 10
ORDER = 512
SLOTS = 4
HALF = BS // 2
MESH = pl.DeviceIdType.MESH
F32 = jnp.float32
BF16 = jnp.bfloat16
PAIRS = [(a, b) for a in range(NB) for b in range(a, NB)]
NO_PART = NPS


def mm(a, b):
    return jnp.dot(a, b, preferred_element_type=F32)


def eye(order, value):
    r = lax.broadcasted_iota(jnp.int32, (order, order), 0)
    c = lax.broadcasted_iota(jnp.int32, (order, order), 1)
    return jnp.where(r == c, value, 0.0)


def mean_diagonal(m):
    total = None
    for a in range(NB):
        s = slice(a * BS, (a + 1) * BS)
        r = lax.broadcasted_iota(jnp.int32, (BS, BS), 0)
        c = lax.broadcasted_iota(jnp.int32, (BS, BS), 1)
        part = jnp.where(r == c, m[s, s], 0.0)
        total = part if total is None else total + part
    return jnp.sum(total, keepdims=True) * (1.0 / ORDER)


def kernel(
    n_slab,
    hb_ref,
    ids_hbm,
    w_hbm,
    mu_ref,
    dens_ref,
    energy_ref,
    near,
    parts0,
    parts1,
    parts2,
    parts3,
    ids_ref,
    w_ref,
    remote_ids,
    inverse,
    h_mat,
    sums,
    far,
    got,
    local_sem,
    small_sem,
    gather_send,
    gather_recv,
    ids_send,
    ids_recv,
    part_send,
    part_recv,
    sum_send,
    sum_recv,
):
    slab = lax.axis_index("slab")
    layer = lax.axis_index("layer")
    core = lax.rem(slab, 2)
    partner_slab = slab + 1 - 2 * core
    other_slab = lax.rem(slab - 1 + 2 * core + n_slab, n_slab)
    up_layer = lax.rem(layer + 1, 4)
    down_layer = lax.rem(layer + 3, 4)
    far_layer = lax.rem(layer + 2, 4)
    up, down = (slab, up_layer), (slab, down_layer)
    partner, other = (partner_slab, layer), (other_slab, layer)
    parts = (parts0, parts1, parts2, parts3)

    def remote(src, dst, send, recv, device):
        return pltpu.make_async_remote_copy(
            src_ref=src, dst_ref=dst, send_sem=send, recv_sem=recv, device_id=device, device_id_type=MESH
        )

    barrier = pltpu.get_barrier_semaphore()
    for device in (other, up, down, partner):
        pl.semaphore_signal(barrier, inc=1, device_id=device, device_id_type=MESH)
    locals_ = [pltpu.make_async_copy(hb_ref, near.at[pl.ds(layer * SLOTS, SLOTS)], local_sem)]
    for i, (src, dst) in enumerate(((ids_hbm, ids_ref), (w_hbm, w_ref))):
        locals_.append(pltpu.make_async_copy(src, dst, small_sem.at[i]))
    for c in locals_:
        c.start()
    zero_block = jnp.zeros((HALF, BS), BF16)
    for part in parts:
        for j in range(3):
            part[j, NO_PART] = zero_block
    pl.semaphore_wait(barrier, 4)

    def piece(group, which_layer, first, count):
        return near.at[pl.ds(group * 16 + which_layer * SLOTS + first, count)]

    started = []

    def send(src, group, which_layer, first, count, index, device):
        c = remote(src, piece(group, which_layer, first, count), gather_send.at[index], gather_recv.at[index], device)
        c.start()
        started.append(c)

    def wait_recv(group, which_layer, first, count, index):
        at = piece(group, which_layer, first, count)
        remote(at, at, gather_send.at[index], gather_recv.at[index], up).wait_recv()

    send(hb_ref.at[pl.ds(0, 2)], 0, layer, 0, 2, 0, up)
    send(hb_ref.at[pl.ds(2, 2)], 0, layer, 2, 2, 1, down)
    send(hb_ref, 2, layer, 0, 4, 2, other)
    send(hb_ref.at[pl.ds(2, 2)], 0, layer, 2, 2, 3, up)
    send(hb_ref.at[pl.ds(0, 2)], 0, layer, 0, 2, 4, down)
    send(hb_ref, 1, layer, 0, 4, 5, partner)
    ids_copies = []
    for j, device in enumerate((partner, other)):
        ids_copies.append(remote(ids_hbm, remote_ids.at[j], ids_send.at[j], ids_recv.at[j], device))
        ids_copies[-1].start()

    relays = (
        (down_layer, 0, 0, 6, up),
        (up_layer, 2, 1, 7, down),
        (down_layer, 2, 3, None, None),
        (up_layer, 0, 4, None, None),
        (far_layer, 0, 6, None, None),
        (far_layer, 2, 7, None, None),
    )
    for i, (which, first, index, onward, device) in enumerate(relays):
        wait_recv(0, which, first, 2, index)
        if onward is not None:
            send(piece(0, which, first, 2), 0, which, first, 2, onward, device)
        send(piece(0, which, first, 2), 2, which, first, 2, 8 + i, other)
        send(piece(0, which, first, 2), 1, which, first, 2, 14 + i, partner)

    for c in locals_:
        c.wait()
    for c in ids_copies:
        c.wait_recv()

    def find(s, _):
        want = slab * 16 + s
        found = [NO_PART + 0 * want for _ in range(3)]
        for k in range(NPS):
            found[0] = jnp.where(ids_ref[0, k] == want, k, found[0])
            found[1] = jnp.where(remote_ids[0, 0, k] == want, k, found[1])
            found[2] = jnp.where(remote_ids[1, 0, k] == want, k, found[2])
        for j in range(3):
            inverse[j, s] = found[j]
        return 0

    lax.fori_loop(0, 16, find, 0)

    wait_recv(1, layer, 0, 4, 5)
    wait_recv(2, layer, 0, 4, 2)
    for i, (which, first, _, _, _) in enumerate(relays):
        wait_recv(1, which, first, 2, 14 + i)
        wait_recv(2, which, first, 2, 8 + i)

    for k, (a, b) in enumerate(PAIRS):
        request = ids_ref[0, k]
        its_slab = request // 16
        group = jnp.where(its_slab == slab, 0, jnp.where(its_slab == partner_slab, 1, 2))
        block = near[group * 16 + request - its_slab * 16].astype(F32)
        ra, rb = pl.ds(a * BS, BS), pl.ds(b * BS, BS)
        if a == b:
            h_mat[ra, ra] = block + block.T
        else:
            h_mat[ra, rb] = block
            h_mat[rb, ra] = block.T
    h = h_mat[...]
    mu = mu_ref[0]
    norm2 = jnp.zeros((BS, BS), F32)
    for a in range(NB):
        for b in range(NB):
            block = h[a * BS : (a + 1) * BS, b * BS : (b + 1) * BS]
            if a == b:
                block = eye(BS, mu) - block
            norm2 += block * block
    norm2 = jnp.sum(norm2, keepdims=True) * (1.0 / ORDER) + 1e-06
    inv = 0.5 * lax.rsqrt(norm2)
    hb = h.astype(BF16)
    x0 = mu * inv
    s0 = (inv * inv) * mm(hb, hb) - (2.0 * x0 * inv) * h + eye(ORDER, x0 * x0 - 0.25)
    x1 = (-1.375 * inv) * h - (0.5 * x0) * s0 + (0.5 * inv) * mm(hb, s0.astype(BF16)) + eye(ORDER, 1.375 * x0)
    t1 = mean_diagonal(x1)
    b1 = x1 - eye(ORDER, t1)
    b1h = b1.astype(BF16)
    s1 = mm(b1h, b1h) + (2.0 * t1) * b1 + eye(ORDER, t1 * t1)
    u1 = mean_diagonal(s1)
    s1 = s1 - eye(ORDER, u1)
    x2 = (1.5 - 0.5 * u1) * x1 - (0.5 * t1) * s1 - 0.5 * mm(b1h, s1.astype(BF16))

    weights = [0.5 * w_ref[0, k] for k in range(NPS)]
    part_copies = []

    def store_parts(matrix, chunk, half, identity):
        for k, (a, b) in enumerate(PAIRS):
            first = a * BS + half * HALF
            block = matrix[first : first + HALF, b * BS : (b + 1) * BS]
            if identity and a == b:
                r = lax.broadcasted_iota(jnp.int32, (HALF, BS), 0) + half * HALF
                c = lax.broadcasted_iota(jnp.int32, (HALF, BS), 1)
                block = block + jnp.where(r == c, 1.0, 0.0)
            parts[chunk][0, k] = (weights[k] * block).astype(BF16)
        for j, device in ((2, other), (1, partner)):
            c = remote(
                parts[chunk].at[0, pl.ds(0, NPS)],
                parts[chunk].at[j, pl.ds(0, NPS)],
                part_send.at[2 * chunk + j - 1],
                part_recv.at[2 * chunk + j - 1],
                device,
            )
            c.start()
            part_copies.append(c)

    store_parts(x2, 0, 0, True)
    store_parts(x2, 1, 1, True)

    t2 = mean_diagonal(x2)
    c2 = x2 - eye(ORDER, t2)
    c2h = c2.astype(BF16)
    c2l = (c2 - c2h.astype(F32)).astype(BF16)
    hl = (h - hb.astype(F32)).astype(BF16)
    e2 = (1.0 + t2) * h + mm(c2h, hb) + mm(c2l, hb) + mm(c2h, hl)
    store_parts(e2, 2, 0, False)
    store_parts(e2, 3, 1, False)

    sum_copies = []
    outs = (dens_ref, energy_ref)

    def collect(chunk, which_layer, j):
        s = which_layer * SLOTS + j
        part = parts[chunk]
        return (
            part[0, inverse[0, s]].astype(F32)
            + part[1, inverse[1, s]].astype(F32)
            + part[2, inverse[2, s]].astype(F32)
        )

    def move(src, dst, index, device):
        c = remote(src, dst, sum_send.at[index], sum_recv.at[index], device)
        c.start()
        sum_copies.append(c)
        return c

    def first_hop(chunk):
        part_copies[2 * chunk].wait_recv()
        part_copies[2 * chunk + 1].wait_recv()
        for j in range(4):
            sums[chunk, 2, j] = collect(chunk, far_layer, j).astype(BF16)
        to_up = move(sums.at[chunk, 2, pl.ds(0, 2)], far.at[chunk, 0], 4 * chunk, up)
        to_down = move(sums.at[chunk, 2, pl.ds(2, 2)], far.at[chunk, 1], 4 * chunk + 1, down)
        for j in range(2):
            sums[chunk, 0, 2 + j] = collect(chunk, up_layer, 2 + j).astype(BF16)
            sums[chunk, 1, j] = collect(chunk, down_layer, j).astype(BF16)
        return to_up, to_down

    def second_hop(chunk, arrivals):
        arrivals[0].wait_recv()
        for j in range(2):
            sums[chunk, 0, j] = (collect(chunk, up_layer, j) + far[chunk, 0, j].astype(F32)).astype(BF16)
        to_up = move(sums.at[chunk, 0], got.at[chunk, 0], 4 * chunk + 2, up)
        arrivals[1].wait_recv()
        for j in range(2):
            sums[chunk, 1, 2 + j] = (collect(chunk, down_layer, 2 + j) + far[chunk, 1, j].astype(F32)).astype(BF16)
        to_down = move(sums.at[chunk, 1], got.at[chunk, 1], 4 * chunk + 3, down)
        return to_up, to_down

    def finish(chunk, arrivals):
        for c in arrivals:
            c.wait_recv()
        rows = pl.ds((chunk % 2) * HALF, HALF)
        for j in range(4):
            outs[chunk // 2][j, rows] = collect(chunk, layer, j) + (
                got[chunk, 0, j].astype(F32) + got[chunk, 1, j].astype(F32)
            )

    ready = {0: first_hop(0)}
    done = {}
    for chunk in range(1, 4):
        ready[chunk] = first_hop(chunk)
        done[chunk - 1] = second_hop(chunk - 1, ready[chunk - 1])
    done[3] = second_hop(3, ready[3])
    for chunk in range(4):
        finish(chunk, done[chunk])

    for c in ids_copies + started + part_copies + sum_copies:
        c.wait_send()


def write_out(dens_ref, energy_ref, dens_out, energy_out, sems):
    copies = [
        pltpu.make_async_copy(dens_ref, dens_out, sems.at[0]),
        pltpu.make_async_copy(energy_ref, energy_out, sems.at[1]),
    ]
    for c in copies:
        c.start()
    for c in copies:
        c.wait()


def solution(mesh):
    n_slab = mesh.shape["slab"]

    def step(hamilton_blocks, pair_ids, weights, potential):
        hbm = pl.BlockSpec(memory_space=pltpu.HBM)
        vmem = pl.BlockSpec(memory_space=pltpu.VMEM)
        dma = pltpu.SemaphoreType.DMA
        out = jax.ShapeDtypeStruct((SLOTS, BS, BS), F32)
        sums = pl.pallas_call(
            functools.partial(kernel, n_slab),
            out_shape=(pltpu.VMEM(out.shape, F32), pltpu.VMEM(out.shape, F32)),
            in_specs=[hbm, hbm, hbm, pl.BlockSpec(memory_space=pltpu.SMEM)],
            out_specs=(vmem, vmem),
            scratch_shapes=[
                pltpu.VMEM((48, BS, BS), BF16),
                *[pltpu.VMEM((3, NPS + 1, HALF, BS), BF16)] * 4,
                pltpu.SMEM((1, NPS), jnp.int32),
                pltpu.SMEM((1, NPS), F32),
                pltpu.SMEM((2, 1, NPS), jnp.int32),
                pltpu.SMEM((3, 16), jnp.int32),
                pltpu.VMEM((ORDER, ORDER), F32),
                pltpu.VMEM((4, 3, SLOTS, HALF, BS), BF16),
                pltpu.VMEM((4, 2, 2, HALF, BS), BF16),
                pltpu.VMEM((4, 2, SLOTS, HALF, BS), BF16),
                dma,
                dma((2,)),
                dma((20,)),
                dma((20,)),
                dma((2,)),
                dma((2,)),
                dma((8,)),
                dma((8,)),
                dma((16,)),
                dma((16,)),
            ],
            compiler_params=pltpu.CompilerParams(
                collective_id=0, has_side_effects=True, vmem_limit_bytes=48 * 1024 * 1024
            ),
        )(*[pltpu.with_memory_space_constraint(x, pltpu.HBM) for x in (hamilton_blocks, pair_ids, weights)], potential)
        return pl.pallas_call(
            write_out,
            out_shape=(pltpu.HBM(out.shape, F32), pltpu.HBM(out.shape, F32)),
            in_specs=[vmem, vmem],
            out_specs=(hbm, hbm),
            scratch_shapes=[dma((2,))],
        )(*[pltpu.with_memory_space_constraint(x, pltpu.VMEM) for x in sums])

    return jax.shard_map(
        step,
        mesh=mesh,
        in_specs=(P(("slab", "layer"), None, None), P(("slab", "layer"), None), P(("slab", "layer"), None), P()),
        out_specs=(P(("slab", "layer"), None, None), P(("slab", "layer"), None, None)),
        check_vma=False,
    )
```

```python
import functools

import jax
import jax.numpy as jnp
import numpy as np
from jax import lax
from jax.experimental import pallas as pl
from jax.experimental.pallas import tpu as pltpu
from jax.sharding import PartitionSpec as P

BS = 128
NB = 4
NPS = 10
ORDER = 512
SLOTS = 4
ROWS = 32
CHUNKS = tuple((energy, row, ROWS) for energy in range(2) for row in range(0, BS, ROWS))
N_CHUNK = len(CHUNKS)
MESH = pl.DeviceIdType.MESH
F32 = jnp.float32
BF16 = jnp.bfloat16
PAIRS = [(a, b) for a in range(NB) for b in range(a, NB)]
NO_PART = NPS


def mm(a, b):
    return jnp.dot(a, b, preferred_element_type=F32)


def eye(order, value):
    r = lax.broadcasted_iota(jnp.int32, (order, order), 0)
    c = lax.broadcasted_iota(jnp.int32, (order, order), 1)
    return jnp.where(r == c, value, 0.0)


def mean_diagonal(m):
    total = None
    for a in range(NB):
        s = slice(a * BS, (a + 1) * BS)
        r = lax.broadcasted_iota(jnp.int32, (BS, BS), 0)
        c = lax.broadcasted_iota(jnp.int32, (BS, BS), 1)
        part = jnp.where(r == c, m[s, s], 0.0)
        total = part if total is None else total + part
    return jnp.sum(total, keepdims=True) * (1.0 / ORDER)


def kernel(n_slab, hb_ref, ids_hbm, w_hbm, mu_ref, dens_ref, energy_ref, near, *rest):
    parts, sums, got = (rest[i * N_CHUNK : (i + 1) * N_CHUNK] for i in range(3))
    ids_ref, w_ref, remote_ids, inverse, h_mat, local_sem, small_sem = rest[3 * N_CHUNK : 3 * N_CHUNK + 7]
    gather_send, gather_recv, ids_send, ids_recv, part_send, part_recv, sum_send, sum_recv = rest[3 * N_CHUNK + 7 :]
    outs = (dens_ref, energy_ref)
    slab = lax.axis_index("slab")
    layer = lax.axis_index("layer")
    core = lax.rem(slab, 2)
    partner_slab = slab + 1 - 2 * core
    other_slab = lax.rem(slab - 1 + 2 * core + n_slab, n_slab)
    up_layer = lax.rem(layer + 1, 4)
    down_layer = lax.rem(layer + 3, 4)
    far_layer = lax.rem(layer + 2, 4)
    up, down = (slab, up_layer), (slab, down_layer)
    partner, other, across = (partner_slab, layer), (other_slab, layer), (slab, far_layer)

    def remote(src, dst, send, recv, device):
        return pltpu.make_async_remote_copy(
            src_ref=src, dst_ref=dst, send_sem=send, recv_sem=recv, device_id=device, device_id_type=MESH
        )

    barrier = pltpu.get_barrier_semaphore()
    for device in (other, up, down, partner, across):
        pl.semaphore_signal(barrier, inc=1, device_id=device, device_id_type=MESH)
    locals_ = [pltpu.make_async_copy(hb_ref, near.at[pl.ds(layer * SLOTS, SLOTS)], local_sem)]
    for i, (src, dst) in enumerate(((ids_hbm, ids_ref), (w_hbm, w_ref))):
        locals_.append(pltpu.make_async_copy(src, dst, small_sem.at[i]))
    for c in locals_:
        c.start()
    for (_, _, rows), part in zip(CHUNKS, parts):
        for j in range(3):
            part[j, NO_PART] = jnp.zeros((rows, BS), BF16)
    pl.semaphore_wait(barrier, 5)

    def piece(group, which_layer, first, count):
        return near.at[pl.ds(group * 16 + which_layer * SLOTS + first, count)]

    started = []

    def send(src, group, which_layer, first, count, index, device):
        c = remote(src, piece(group, which_layer, first, count), gather_send.at[index], gather_recv.at[index], device)
        c.start()
        started.append(c)

    def wait_recv(group, which_layer, first, count, index):
        at = piece(group, which_layer, first, count)
        remote(at, at, gather_send.at[index], gather_recv.at[index], up).wait_recv()

    send(hb_ref.at[pl.ds(0, 2)], 0, layer, 0, 2, 0, up)
    send(hb_ref.at[pl.ds(2, 2)], 0, layer, 2, 2, 1, down)
    send(hb_ref, 2, layer, 0, 4, 2, other)
    send(hb_ref.at[pl.ds(2, 2)], 0, layer, 2, 2, 3, up)
    send(hb_ref.at[pl.ds(0, 2)], 0, layer, 0, 2, 4, down)
    send(hb_ref, 1, layer, 0, 4, 5, partner)
    send(hb_ref.at[pl.ds(0, 2)], 0, layer, 0, 2, 6, across)
    send(hb_ref.at[pl.ds(2, 2)], 0, layer, 2, 2, 7, across)
    ids_copies = []
    for j, device in enumerate((partner, other)):
        ids_copies.append(remote(ids_hbm, remote_ids.at[j], ids_send.at[j], ids_recv.at[j], device))
        ids_copies[-1].start()

    relays = (
        (down_layer, 0, 0),
        (up_layer, 2, 1),
        (down_layer, 2, 3),
        (up_layer, 0, 4),
        (far_layer, 0, 6),
        (far_layer, 2, 7),
    )
    for i, (which, first, index) in enumerate(relays):
        wait_recv(0, which, first, 2, index)
        send(piece(0, which, first, 2), 2, which, first, 2, 8 + i, other)
        send(piece(0, which, first, 2), 1, which, first, 2, 14 + i, partner)

    for c in locals_:
        c.wait()
    for c in ids_copies:
        c.wait_recv()

    def find(s, _):
        want = slab * 16 + s
        found = [NO_PART + 0 * want for _ in range(3)]
        for k in range(NPS):
            found[0] = jnp.where(ids_ref[0, k] == want, k, found[0])
            found[1] = jnp.where(remote_ids[0, 0, k] == want, k, found[1])
            found[2] = jnp.where(remote_ids[1, 0, k] == want, k, found[2])
        for j in range(3):
            inverse[j, s] = found[j]
        return 0

    lax.fori_loop(0, 16, find, 0)

    wait_recv(1, layer, 0, 4, 5)
    wait_recv(2, layer, 0, 4, 2)
    for i, (which, first, _) in enumerate(relays):
        wait_recv(1, which, first, 2, 14 + i)
        wait_recv(2, which, first, 2, 8 + i)

    for k, (a, b) in enumerate(PAIRS):
        request = ids_ref[0, k]
        its_slab = request // 16
        group = jnp.where(its_slab == slab, 0, jnp.where(its_slab == partner_slab, 1, 2))
        block = near[group * 16 + request - its_slab * 16].astype(F32)
        ra, rb = pl.ds(a * BS, BS), pl.ds(b * BS, BS)
        if a == b:
            h_mat[ra, ra] = block + block.T
        else:
            h_mat[ra, rb] = block
            h_mat[rb, ra] = block.T
    h = h_mat[...]
    mu = mu_ref[0]
    norm2 = jnp.zeros((BS, BS), F32)
    for a in range(NB):
        for b in range(NB):
            block = h[a * BS : (a + 1) * BS, b * BS : (b + 1) * BS]
            if a == b:
                block = eye(BS, mu) - block
            norm2 += block * block
    norm2 = jnp.sum(norm2, keepdims=True) * (1.0 / ORDER) + 1e-06
    inv = 0.5 * lax.rsqrt(norm2)
    hb = h.astype(BF16)
    x0 = mu * inv
    s0 = (inv * inv) * mm(hb, hb) - (2.0 * x0 * inv) * h + eye(ORDER, x0 * x0 - 0.25)
    x1 = (-1.375 * inv) * h - (0.5 * x0) * s0 + (0.5 * inv) * mm(hb, s0.astype(BF16)) + eye(ORDER, 1.375 * x0)
    t1 = mean_diagonal(x1)
    b1 = x1 - eye(ORDER, t1)
    b1h = b1.astype(BF16)
    s1 = mm(b1h, b1h) + (2.0 * t1) * b1 + eye(ORDER, t1 * t1)
    u1 = mean_diagonal(s1)
    s1 = s1 - eye(ORDER, u1)
    x2 = (1.5 - 0.5 * u1) * x1 - (0.5 * t1) * s1 - 0.5 * mm(b1h, s1.astype(BF16))

    weights = [0.5 * w_ref[0, k] for k in range(NPS)]
    part_copies = []

    def store_parts(matrix, chunk):
        energy, row, rows = CHUNKS[chunk]
        for k, (a, b) in enumerate(PAIRS):
            first = a * BS + row
            block = matrix[first : first + rows, b * BS : (b + 1) * BS]
            if not energy and a == b:
                r = lax.broadcasted_iota(jnp.int32, (rows, BS), 0) + row
                c = lax.broadcasted_iota(jnp.int32, (rows, BS), 1)
                block = block + jnp.where(r == c, 1.0, 0.0)
            parts[chunk][0, k] = (weights[k] * block).astype(BF16)
        for j, device in ((2, other), (1, partner)):
            c = remote(
                parts[chunk].at[0, pl.ds(0, NPS)],
                parts[chunk].at[j, pl.ds(0, NPS)],
                part_send.at[2 * chunk + j - 1],
                part_recv.at[2 * chunk + j - 1],
                device,
            )
            c.start()
            part_copies.append(c)

    for chunk in range(N_CHUNK):
        if not CHUNKS[chunk][0]:
            store_parts(x2, chunk)

    t2 = mean_diagonal(x2)
    c2 = x2 - eye(ORDER, t2)
    c2h = c2.astype(BF16)
    c2l = (c2 - c2h.astype(F32)).astype(BF16)
    hl = (h - hb.astype(F32)).astype(BF16)
    e2 = (1.0 + t2) * h + mm(c2h, hb) + mm(c2l, hb) + mm(c2h, hl)
    for chunk in range(N_CHUNK):
        if CHUNKS[chunk][0]:
            store_parts(e2, chunk)

    sum_copies = []

    def collect(chunk, which_layer, j):
        s = which_layer * SLOTS + j
        part = parts[chunk]
        return (
            part[0, inverse[0, s]].astype(F32)
            + part[1, inverse[1, s]].astype(F32)
            + part[2, inverse[2, s]].astype(F32)
        )

    for chunk in range(N_CHUNK):
        part_copies[2 * chunk].wait_recv()
        part_copies[2 * chunk + 1].wait_recv()
        for i, (which, device) in enumerate(((far_layer, across), (up_layer, up), (down_layer, down))):
            for j in range(SLOTS):
                sums[chunk][i, j] = collect(chunk, which, j).astype(BF16)
            index = 3 * chunk + i
            sum_copies.append(
                remote(sums[chunk].at[i], got[chunk].at[i], sum_send.at[index], sum_recv.at[index], device)
            )
            sum_copies[-1].start()

    for chunk, (energy, row, rows) in enumerate(CHUNKS):
        for i in range(3):
            sum_copies[3 * chunk + i].wait_recv()
        for j in range(SLOTS):
            outs[energy][j, pl.ds(row, rows)] = collect(chunk, layer, j) + (
                got[chunk][0, j].astype(F32) + got[chunk][1, j].astype(F32) + got[chunk][2, j].astype(F32)
            )

    for c in ids_copies + started + part_copies + sum_copies:
        c.wait_send()


def write_out(dens_ref, energy_ref, dens_out, energy_out, sems):
    copies = [
        pltpu.make_async_copy(dens_ref, dens_out, sems.at[0]),
        pltpu.make_async_copy(energy_ref, energy_out, sems.at[1]),
    ]
    for c in copies:
        c.start()
    for c in copies:
        c.wait()


def solution(mesh):
    n_slab = mesh.shape["slab"]

    def step(hamilton_blocks, pair_ids, weights, potential):
        hbm = pl.BlockSpec(memory_space=pltpu.HBM)
        vmem = pl.BlockSpec(memory_space=pltpu.VMEM)
        dma = pltpu.SemaphoreType.DMA
        out = jax.ShapeDtypeStruct((SLOTS, BS, BS), F32)
        sums = pl.pallas_call(
            functools.partial(kernel, n_slab),
            out_shape=(pltpu.VMEM(out.shape, F32), pltpu.VMEM(out.shape, F32)),
            in_specs=[hbm, hbm, hbm, pl.BlockSpec(memory_space=pltpu.SMEM)],
            out_specs=(vmem, vmem),
            scratch_shapes=[
                pltpu.VMEM((48, BS, BS), BF16),
                *[pltpu.VMEM((3, NPS + 1, rows, BS), BF16) for _, _, rows in CHUNKS],
                *[pltpu.VMEM((3, SLOTS, rows, BS), BF16) for _, _, rows in CHUNKS],
                *[pltpu.VMEM((3, SLOTS, rows, BS), BF16) for _, _, rows in CHUNKS],
                pltpu.SMEM((1, NPS), jnp.int32),
                pltpu.SMEM((1, NPS), F32),
                pltpu.SMEM((2, 1, NPS), jnp.int32),
                pltpu.SMEM((3, 16), jnp.int32),
                pltpu.VMEM((ORDER, ORDER), F32),
                dma,
                dma((2,)),
                dma((20,)),
                dma((20,)),
                dma((2,)),
                dma((2,)),
                dma((2 * N_CHUNK,)),
                dma((2 * N_CHUNK,)),
                dma((3 * N_CHUNK,)),
                dma((3 * N_CHUNK,)),
            ],
            compiler_params=pltpu.CompilerParams(
                collective_id=0, has_side_effects=True, vmem_limit_bytes=48 * 1024 * 1024
            ),
        )(*[pltpu.with_memory_space_constraint(x, pltpu.HBM) for x in (hamilton_blocks, pair_ids, weights)], potential)
        return pl.pallas_call(
            write_out,
            out_shape=(pltpu.HBM(out.shape, F32), pltpu.HBM(out.shape, F32)),
            in_specs=[vmem, vmem],
            out_specs=(hbm, hbm),
            scratch_shapes=[dma((2,))],
        )(*[pltpu.with_memory_space_constraint(x, pltpu.VMEM) for x in sums])

    return jax.shard_map(
        step,
        mesh=mesh,
        in_specs=(P(("slab", "layer"), None, None), P(("slab", "layer"), None), P(("slab", "layer"), None), P()),
        out_specs=(P(("slab", "layer"), None, None), P(("slab", "layer"), None, None)),
        check_vma=False,
    )
```

```python
import functools

import jax
import jax.numpy as jnp
import numpy as np
from jax import lax
from jax.experimental import pallas as pl
from jax.experimental.pallas import tpu as pltpu
from jax.sharding import PartitionSpec as P

BS = 128
NB = 4
NPS = 10
ORDER = 512
SLOTS = 4
ROWS = 32
CHUNKS = tuple((energy, row, ROWS) for energy in range(2) for row in range(0, BS, ROWS))
N_CHUNK = len(CHUNKS)
MESH = pl.DeviceIdType.MESH
F32 = jnp.float32
BF16 = jnp.bfloat16
PAIRS = [(a, b) for a in range(NB) for b in range(a, NB)]
NO_PART = NPS


def mm(a, b):
    return jnp.dot(a, b, preferred_element_type=F32)


def eye(order, value):
    r = lax.broadcasted_iota(jnp.int32, (order, order), 0)
    c = lax.broadcasted_iota(jnp.int32, (order, order), 1)
    return jnp.where(r == c, value, 0.0)


def mean_square(m, n):
    total = jnp.zeros((BS, BS), F32)
    for a in range(NB):
        for b in range(NB):
            s, t = slice(a * BS, (a + 1) * BS), slice(b * BS, (b + 1) * BS)
            total += m[s, t] * n[s, t]
    return jnp.sum(total, keepdims=True) * (1.0 / ORDER)


def mean_diagonal(m):
    total = None
    for a in range(NB):
        s = slice(a * BS, (a + 1) * BS)
        r = lax.broadcasted_iota(jnp.int32, (BS, BS), 0)
        c = lax.broadcasted_iota(jnp.int32, (BS, BS), 1)
        part = jnp.where(r == c, m[s, s], 0.0)
        total = part if total is None else total + part
    return jnp.sum(total, keepdims=True) * (1.0 / ORDER)


def kernel(n_slab, hb_ref, ids_hbm, w_hbm, mu_ref, dens_ref, energy_ref, near, *rest):
    parts, sums, got = (rest[i * N_CHUNK : (i + 1) * N_CHUNK] for i in range(3))
    ids_ref, w_ref, remote_ids, inverse, h_mat, local_sem, small_sem = rest[3 * N_CHUNK : 3 * N_CHUNK + 7]
    gather_send, gather_recv, ids_send, ids_recv, part_send, part_recv, sum_send, sum_recv = rest[3 * N_CHUNK + 7 :]
    outs = (dens_ref, energy_ref)
    slab = lax.axis_index("slab")
    layer = lax.axis_index("layer")
    core = lax.rem(slab, 2)
    partner_slab = slab + 1 - 2 * core
    other_slab = lax.rem(slab - 1 + 2 * core + n_slab, n_slab)
    up_layer = lax.rem(layer + 1, 4)
    down_layer = lax.rem(layer + 3, 4)
    far_layer = lax.rem(layer + 2, 4)
    up, down = (slab, up_layer), (slab, down_layer)
    partner, other, across = (partner_slab, layer), (other_slab, layer), (slab, far_layer)

    def remote(src, dst, send, recv, device):
        return pltpu.make_async_remote_copy(
            src_ref=src, dst_ref=dst, send_sem=send, recv_sem=recv, device_id=device, device_id_type=MESH
        )

    barrier = pltpu.get_barrier_semaphore()
    for device in (other, up, down, partner, across):
        pl.semaphore_signal(barrier, inc=1, device_id=device, device_id_type=MESH)
    locals_ = [pltpu.make_async_copy(hb_ref, near.at[pl.ds(layer * SLOTS, SLOTS)], local_sem)]
    for i, (src, dst) in enumerate(((ids_hbm, ids_ref), (w_hbm, w_ref))):
        locals_.append(pltpu.make_async_copy(src, dst, small_sem.at[i]))
    for c in locals_:
        c.start()
    for (_, _, rows), part in zip(CHUNKS, parts):
        for j in range(3):
            part[j, NO_PART] = jnp.zeros((rows, BS), BF16)
    pl.semaphore_wait(barrier, 5)

    def piece(group, which_layer, first, count):
        return near.at[pl.ds(group * 16 + which_layer * SLOTS + first, count)]

    started = []

    def send(src, group, which_layer, first, count, index, device):
        c = remote(src, piece(group, which_layer, first, count), gather_send.at[index], gather_recv.at[index], device)
        c.start()
        started.append(c)

    def wait_recv(group, which_layer, first, count, index):
        at = piece(group, which_layer, first, count)
        remote(at, at, gather_send.at[index], gather_recv.at[index], up).wait_recv()

    locals_[0].wait()
    send(piece(0, layer, 0, 2), 0, layer, 0, 2, 0, up)
    send(piece(0, layer, 2, 2), 0, layer, 2, 2, 1, down)
    send(piece(0, layer, 0, 4), 2, layer, 0, 4, 2, other)
    send(piece(0, layer, 2, 2), 0, layer, 2, 2, 3, up)
    send(piece(0, layer, 0, 2), 0, layer, 0, 2, 4, down)
    send(piece(0, layer, 0, 4), 1, layer, 0, 4, 5, partner)
    send(piece(0, layer, 0, 2), 0, layer, 0, 2, 6, across)
    send(piece(0, layer, 2, 2), 0, layer, 2, 2, 7, across)
    ids_copies = []
    for j, device in enumerate((partner, other)):
        ids_copies.append(remote(ids_hbm, remote_ids.at[j], ids_send.at[j], ids_recv.at[j], device))
        ids_copies[-1].start()

    relays = (
        (down_layer, 0, 0),
        (up_layer, 2, 1),
        (down_layer, 2, 3),
        (up_layer, 0, 4),
        (far_layer, 0, 6),
        (far_layer, 2, 7),
    )
    for i, (which, first, index) in enumerate(relays):
        wait_recv(0, which, first, 2, index)
        send(piece(0, which, first, 2), 2, which, first, 2, 8 + i, other)
        send(piece(0, which, first, 2), 1, which, first, 2, 14 + i, partner)

    for c in locals_[1:]:
        c.wait()
    for c in ids_copies:
        c.wait_recv()

    def find(s, _):
        want = slab * 16 + s
        found = [NO_PART + 0 * want for _ in range(3)]
        for k in range(NPS):
            found[0] = jnp.where(ids_ref[0, k] == want, k, found[0])
            found[1] = jnp.where(remote_ids[0, 0, k] == want, k, found[1])
            found[2] = jnp.where(remote_ids[1, 0, k] == want, k, found[2])
        for j in range(3):
            inverse[j, s] = found[j]
        return 0

    lax.fori_loop(0, 16, find, 0)

    wait_recv(1, layer, 0, 4, 5)
    wait_recv(2, layer, 0, 4, 2)
    for i, (which, first, _) in enumerate(relays):
        wait_recv(1, which, first, 2, 14 + i)
        wait_recv(2, which, first, 2, 8 + i)

    for k, (a, b) in enumerate(PAIRS):
        request = ids_ref[0, k]
        its_slab = request // 16
        group = jnp.where(its_slab == slab, 0, jnp.where(its_slab == partner_slab, 1, 2))
        block = near[group * 16 + request - its_slab * 16]
        ra, rb = pl.ds(a * BS, BS), pl.ds(b * BS, BS)
        if a == b:
            h_mat[ra, ra] = block.astype(F32) + block.T.astype(F32)
        else:
            h_mat[ra, rb] = block.astype(F32)
            h_mat[rb, ra] = block.T.astype(F32)
    h = h_mat[...]
    mu = mu_ref[0]
    norm2 = jnp.zeros((BS, BS), F32)
    for a in range(NB):
        for b in range(NB):
            block = h[a * BS : (a + 1) * BS, b * BS : (b + 1) * BS]
            if a == b:
                block = eye(BS, mu) - block
            norm2 += block * block
    norm2 = jnp.sum(norm2, keepdims=True) * (1.0 / ORDER) + 1e-06
    inv = 0.5 * lax.rsqrt(norm2)
    hb = h.astype(BF16)
    x0 = mu * inv
    s0 = (inv * inv) * mm(hb, hb) - (2.0 * x0 * inv) * h + eye(ORDER, x0 * x0 - 0.25)
    x1 = (-1.375 * inv) * h - (0.5 * x0) * s0 + (0.5 * inv) * mm(hb, s0.astype(BF16)) + eye(ORDER, 1.375 * x0)
    t1 = 1.375 * (x0 - inv * mean_diagonal(h)) - (0.5 * x0) * mean_diagonal(s0) + (0.5 * inv) * mean_square(h, s0)
    b1 = x1 - eye(ORDER, t1)
    b1h = b1.astype(BF16)
    u0 = mean_square(b1, b1)
    s1 = mm(b1h, b1h) + (2.0 * t1) * b1 - eye(ORDER, u0)
    u1 = u0 + t1 * t1
    x2 = (1.5 - 0.5 * u1) * x1 - (0.5 * t1) * s1 - 0.5 * mm(b1h, s1.astype(BF16))

    weights = [0.5 * w_ref[0, k] for k in range(NPS)]
    part_copies = []

    def store_parts(matrix, chunk):
        energy, row, rows = CHUNKS[chunk]
        for k, (a, b) in enumerate(PAIRS):
            first = a * BS + row
            block = matrix[first : first + rows, b * BS : (b + 1) * BS]
            if not energy and a == b:
                r = lax.broadcasted_iota(jnp.int32, (rows, BS), 0) + row
                c = lax.broadcasted_iota(jnp.int32, (rows, BS), 1)
                block = block + jnp.where(r == c, 1.0, 0.0)
            parts[chunk][0, k] = (weights[k] * block).astype(BF16)
        for j, device in ((2, other), (1, partner)):
            c = remote(
                parts[chunk].at[0, pl.ds(0, NPS)],
                parts[chunk].at[j, pl.ds(0, NPS)],
                part_send.at[2 * chunk + j - 1],
                part_recv.at[2 * chunk + j - 1],
                device,
            )
            c.start()
            part_copies.append(c)

    for chunk in range(N_CHUNK):
        if not CHUNKS[chunk][0]:
            store_parts(x2, chunk)

    t2 = mean_diagonal(x2)
    c2 = x2 - eye(ORDER, t2)
    c2h = c2.astype(BF16)
    c2l = (c2 - c2h.astype(F32)).astype(BF16)
    hl = (h - hb.astype(F32)).astype(BF16)
    e2 = (1.0 + t2) * h + mm(c2h, hb) + mm(c2l, hb) + mm(c2h, hl)
    for chunk in range(N_CHUNK):
        if CHUNKS[chunk][0]:
            store_parts(e2, chunk)

    sum_copies = []

    def collect(chunk, which_layer, j):
        s = which_layer * SLOTS + j
        part = parts[chunk]
        return (
            part[0, inverse[0, s]].astype(F32)
            + part[1, inverse[1, s]].astype(F32)
            + part[2, inverse[2, s]].astype(F32)
        )

    for chunk in range(N_CHUNK):
        part_copies[2 * chunk].wait_recv()
        part_copies[2 * chunk + 1].wait_recv()
        for i, (which, device) in enumerate(((far_layer, across), (up_layer, up), (down_layer, down))):
            for j in range(SLOTS):
                sums[chunk][i, j] = collect(chunk, which, j).astype(BF16)
            index = 3 * chunk + i
            sum_copies.append(
                remote(sums[chunk].at[i], got[chunk].at[i], sum_send.at[index], sum_recv.at[index], device)
            )
            sum_copies[-1].start()

    for chunk, (energy, row, rows) in enumerate(CHUNKS):
        for i in range(3):
            sum_copies[3 * chunk + i].wait_recv()
        for j in range(SLOTS):
            outs[energy][j, pl.ds(row, rows)] = collect(chunk, layer, j) + (
                got[chunk][0, j].astype(F32) + got[chunk][1, j].astype(F32) + got[chunk][2, j].astype(F32)
            )

    for c in ids_copies + started + part_copies + sum_copies:
        c.wait_send()


def write_out(dens_ref, energy_ref, dens_out, energy_out, sems):
    copies = [
        pltpu.make_async_copy(dens_ref, dens_out, sems.at[0]),
        pltpu.make_async_copy(energy_ref, energy_out, sems.at[1]),
    ]
    for c in copies:
        c.start()
    for c in copies:
        c.wait()


def solution(mesh):
    n_slab = mesh.shape["slab"]

    def step(hamilton_blocks, pair_ids, weights, potential):
        hbm = pl.BlockSpec(memory_space=pltpu.HBM)
        vmem = pl.BlockSpec(memory_space=pltpu.VMEM)
        dma = pltpu.SemaphoreType.DMA
        out = jax.ShapeDtypeStruct((SLOTS, BS, BS), F32)
        sums = pl.pallas_call(
            functools.partial(kernel, n_slab),
            out_shape=(pltpu.VMEM(out.shape, F32), pltpu.VMEM(out.shape, F32)),
            in_specs=[hbm, hbm, hbm, pl.BlockSpec(memory_space=pltpu.SMEM)],
            out_specs=(vmem, vmem),
            scratch_shapes=[
                pltpu.VMEM((48, BS, BS), BF16),
                *[pltpu.VMEM((3, NPS + 1, rows, BS), BF16) for _, _, rows in CHUNKS],
                *[pltpu.VMEM((3, SLOTS, rows, BS), BF16) for _, _, rows in CHUNKS],
                *[pltpu.VMEM((3, SLOTS, rows, BS), BF16) for _, _, rows in CHUNKS],
                pltpu.SMEM((1, NPS), jnp.int32),
                pltpu.SMEM((1, NPS), F32),
                pltpu.SMEM((2, 1, NPS), jnp.int32),
                pltpu.SMEM((3, 16), jnp.int32),
                pltpu.VMEM((ORDER, ORDER), F32),
                dma,
                dma((2,)),
                dma((20,)),
                dma((20,)),
                dma((2,)),
                dma((2,)),
                dma((2 * N_CHUNK,)),
                dma((2 * N_CHUNK,)),
                dma((3 * N_CHUNK,)),
                dma((3 * N_CHUNK,)),
            ],
            compiler_params=pltpu.CompilerParams(
                collective_id=0, has_side_effects=True, vmem_limit_bytes=48 * 1024 * 1024
            ),
        )(*[pltpu.with_memory_space_constraint(x, pltpu.HBM) for x in (hamilton_blocks, pair_ids, weights)], potential)
        return pl.pallas_call(
            write_out,
            out_shape=(pltpu.HBM(out.shape, F32), pltpu.HBM(out.shape, F32)),
            in_specs=[vmem, vmem],
            out_specs=(hbm, hbm),
            scratch_shapes=[dma((2,))],
        )(*[pltpu.with_memory_space_constraint(x, pltpu.VMEM) for x in sums])

    return jax.shard_map(
        step,
        mesh=mesh,
        in_specs=(P(("slab", "layer"), None, None), P(("slab", "layer"), None), P(("slab", "layer"), None), P()),
        out_specs=(P(("slab", "layer"), None, None), P(("slab", "layer"), None, None)),
        check_vma=False,
    )
```

```python
import functools

import jax
import jax.numpy as jnp
import numpy as np
from jax import lax
from jax.experimental import pallas as pl
from jax.experimental.pallas import tpu as pltpu
from jax.sharding import PartitionSpec as P

BS = 128
NB = 4
NPS = 10
ORDER = 512
SLOTS = 4
ROWS = 32
AFTER = 1
CHUNKS = tuple((energy, row, ROWS) for energy in range(2) for row in range(0, BS, ROWS))
N_CHUNK = len(CHUNKS)
MESH = pl.DeviceIdType.MESH
F32 = jnp.float32
BF16 = jnp.bfloat16
PAIRS = [(a, b) for a in range(NB) for b in range(a, NB)]
NO_PART = NPS


def mm(a, b):
    return jnp.dot(a, b, preferred_element_type=F32)


def eye(order, value):
    r = lax.broadcasted_iota(jnp.int32, (order, order), 0)
    c = lax.broadcasted_iota(jnp.int32, (order, order), 1)
    return jnp.where(r == c, value, 0.0)


def mean_square(m, n):
    total = jnp.zeros((BS, BS), F32)
    for a in range(NB):
        for b in range(NB):
            s, t = slice(a * BS, (a + 1) * BS), slice(b * BS, (b + 1) * BS)
            total += m[s, t] * n[s, t]
    return jnp.sum(total, keepdims=True) * (1.0 / ORDER)


def mean_diagonal(m):
    total = None
    for a in range(NB):
        s = slice(a * BS, (a + 1) * BS)
        r = lax.broadcasted_iota(jnp.int32, (BS, BS), 0)
        c = lax.broadcasted_iota(jnp.int32, (BS, BS), 1)
        part = jnp.where(r == c, m[s, s], 0.0)
        total = part if total is None else total + part
    return jnp.sum(total, keepdims=True) * (1.0 / ORDER)


def kernel(n_slab, hb_ref, ids_hbm, w_hbm, mu_ref, dens_ref, energy_ref, near, *rest):
    parts, sums, got = (rest[i * N_CHUNK : (i + 1) * N_CHUNK] for i in range(3))
    ids_ref, w_ref, remote_ids, inverse, h_mat, joined, local_sem, small_sem = rest[3 * N_CHUNK : 3 * N_CHUNK + 8]
    gather_send, gather_recv, ids_send, ids_recv, part_send, part_recv, sum_send, sum_recv = rest[3 * N_CHUNK + 8 :]
    outs = (dens_ref, energy_ref)
    slab = lax.axis_index("slab")
    layer = lax.axis_index("layer")
    core = lax.rem(slab, 2)
    partner_slab = slab + 1 - 2 * core
    other_slab = lax.rem(slab - 1 + 2 * core + n_slab, n_slab)
    up_layer = lax.rem(layer + 1, 4)
    down_layer = lax.rem(layer + 3, 4)
    far_layer = lax.rem(layer + 2, 4)
    up, down = (slab, up_layer), (slab, down_layer)
    partner, other, across = (partner_slab, layer), (other_slab, layer), (slab, far_layer)

    def remote(src, dst, send, recv, device):
        return pltpu.make_async_remote_copy(
            src_ref=src, dst_ref=dst, send_sem=send, recv_sem=recv, device_id=device, device_id_type=MESH
        )

    barrier = pltpu.get_barrier_semaphore()
    for device in (up, down, partner, across):
        pl.semaphore_signal(barrier, inc=1, device_id=device, device_id_type=MESH)

    @pl.when(core == 0)
    def _():
        pl.semaphore_signal(barrier, inc=1, device_id=other, device_id_type=MESH)

    locals_ = [pltpu.make_async_copy(hb_ref, near.at[pl.ds(layer * SLOTS, SLOTS)], local_sem)]
    for i, (src, dst) in enumerate(((ids_hbm, ids_ref), (w_hbm, w_ref))):
        locals_.append(pltpu.make_async_copy(src, dst, small_sem.at[i]))
    for c in locals_:
        c.start()
    for (_, _, rows), part in zip(CHUNKS, parts):
        for j in range(3):
            part[j, NO_PART] = jnp.zeros((rows, BS), BF16)
    pl.semaphore_wait(barrier, 4 + core)

    @pl.when(core == 1)
    def _():
        pl.semaphore_signal(joined, inc=1, device_id=other, device_id_type=MESH)


    def piece(group, which_layer, first, count):
        return near.at[pl.ds(group * 16 + which_layer * SLOTS + first, count)]

    started = []

    def send(src, group, which_layer, first, count, index, device):
        c = remote(src, piece(group, which_layer, first, count), gather_send.at[index], gather_recv.at[index], device)
        c.start()
        started.append(c)

    def wait_recv(group, which_layer, first, count, index):
        at = piece(group, which_layer, first, count)
        remote(at, at, gather_send.at[index], gather_recv.at[index], up).wait_recv()

    locals_[0].wait()
    send(piece(0, layer, 0, 2), 0, layer, 0, 2, 0, up)
    send(piece(0, layer, 2, 2), 0, layer, 2, 2, 1, down)
    own_to_other = remote(
        piece(0, layer, 0, 4), piece(2, layer, 0, 4), gather_send.at[2], gather_recv.at[2], other
    )
    started.append(own_to_other)

    @pl.when(core == 1)
    def _():
        own_to_other.start()

    send(piece(0, layer, 2, 2), 0, layer, 2, 2, 3, up)
    send(piece(0, layer, 0, 2), 0, layer, 0, 2, 4, down)
    send(piece(0, layer, 0, 4), 1, layer, 0, 4, 5, partner)
    send(piece(0, layer, 0, 2), 0, layer, 0, 2, 6, across)
    send(piece(0, layer, 2, 2), 0, layer, 2, 2, 7, across)
    ids_copies = [
        remote(ids_hbm, remote_ids.at[j], ids_send.at[j], ids_recv.at[j], device)
        for j, device in enumerate((partner, other))
    ]
    ids_copies[0].start()

    relays = (
        (down_layer, 0, 0),
        (up_layer, 2, 1),
        (down_layer, 2, 3),
        (up_layer, 0, 4),
        (far_layer, 0, 6),
        (far_layer, 2, 7),
    )
    for i, (which, first, index) in enumerate(relays):
        wait_recv(0, which, first, 2, index)
        send(piece(0, which, first, 2), 1, which, first, 2, 14 + i, partner)
        if i == AFTER:

            @pl.when(core == 0)
            def _():
                pl.semaphore_wait(joined, 1)
                own_to_other.start()

            ids_copies[1].start()
        for k in range(i + 1) if i == AFTER else [i] if i > AFTER else []:
            send(piece(0, relays[k][0], relays[k][1], 2), 2, relays[k][0], relays[k][1], 2, 8 + k, other)

    for c in locals_[1:]:
        c.wait()
    for c in ids_copies:
        c.wait_recv()

    def find(s, _):
        want = slab * 16 + s
        found = [NO_PART + 0 * want for _ in range(3)]
        for k in range(NPS):
            found[0] = jnp.where(ids_ref[0, k] == want, k, found[0])
            found[1] = jnp.where(remote_ids[0, 0, k] == want, k, found[1])
            found[2] = jnp.where(remote_ids[1, 0, k] == want, k, found[2])
        for j in range(3):
            inverse[j, s] = found[j]
        return 0

    lax.fori_loop(0, 16, find, 0)

    wait_recv(1, layer, 0, 4, 5)
    wait_recv(2, layer, 0, 4, 2)
    for i, (which, first, _) in enumerate(relays):
        wait_recv(1, which, first, 2, 14 + i)
        wait_recv(2, which, first, 2, 8 + i)

    for k, (a, b) in enumerate(PAIRS):
        request = ids_ref[0, k]
        its_slab = request // 16
        group = jnp.where(its_slab == slab, 0, jnp.where(its_slab == partner_slab, 1, 2))
        block = near[group * 16 + request - its_slab * 16]
        ra, rb = pl.ds(a * BS, BS), pl.ds(b * BS, BS)
        if a == b:
            h_mat[ra, ra] = block.astype(F32) + block.T.astype(F32)
        else:
            h_mat[ra, rb] = block.astype(F32)
            h_mat[rb, ra] = block.T.astype(F32)
    h = h_mat[...]
    mu = mu_ref[0]
    norm2 = jnp.zeros((BS, BS), F32)
    for a in range(NB):
        for b in range(NB):
            block = h[a * BS : (a + 1) * BS, b * BS : (b + 1) * BS]
            if a == b:
                block = eye(BS, mu) - block
            norm2 += block * block
    norm2 = jnp.sum(norm2, keepdims=True) * (1.0 / ORDER) + 1e-06
    inv = 0.5 * lax.rsqrt(norm2)
    hb = h.astype(BF16)
    x0 = mu * inv
    s0 = (inv * inv) * mm(hb, hb) - (2.0 * x0 * inv) * h + eye(ORDER, x0 * x0 - 0.25)
    x1 = (-1.375 * inv) * h - (0.5 * x0) * s0 + (0.5 * inv) * mm(hb, s0.astype(BF16)) + eye(ORDER, 1.375 * x0)
    t1 = 1.375 * (x0 - inv * mean_diagonal(h)) - (0.5 * x0) * mean_diagonal(s0) + (0.5 * inv) * mean_square(h, s0)
    b1 = x1 - eye(ORDER, t1)
    b1h = b1.astype(BF16)
    u0 = mean_square(b1, b1)
    s1 = mm(b1h, b1h) + (2.0 * t1) * b1 - eye(ORDER, u0)
    u1 = u0 + t1 * t1
    x2 = (1.5 - 0.5 * u1) * x1 - (0.5 * t1) * s1 - 0.5 * mm(b1h, s1.astype(BF16))

    weights = [0.5 * w_ref[0, k] for k in range(NPS)]
    part_copies = []

    def store_parts(matrix, chunk):
        energy, row, rows = CHUNKS[chunk]
        for k, (a, b) in enumerate(PAIRS):
            first = a * BS + row
            block = matrix[first : first + rows, b * BS : (b + 1) * BS]
            if not energy and a == b:
                r = lax.broadcasted_iota(jnp.int32, (rows, BS), 0) + row
                c = lax.broadcasted_iota(jnp.int32, (rows, BS), 1)
                block = block + jnp.where(r == c, 1.0, 0.0)
            parts[chunk][0, k] = (weights[k] * block).astype(BF16)
        for j, device in ((2, other), (1, partner)):
            c = remote(
                parts[chunk].at[0, pl.ds(0, NPS)],
                parts[chunk].at[j, pl.ds(0, NPS)],
                part_send.at[2 * chunk + j - 1],
                part_recv.at[2 * chunk + j - 1],
                device,
            )
            c.start()
            part_copies.append(c)

    for chunk in range(N_CHUNK):
        if not CHUNKS[chunk][0]:
            store_parts(x2, chunk)

    t2 = mean_diagonal(x2)
    c2 = x2 - eye(ORDER, t2)
    c2h = c2.astype(BF16)
    c2l = (c2 - c2h.astype(F32)).astype(BF16)
    hl = (h - hb.astype(F32)).astype(BF16)
    e2 = (1.0 + t2) * h + mm(c2h, hb) + mm(c2l, hb) + mm(c2h, hl)
    for chunk in range(N_CHUNK):
        if CHUNKS[chunk][0]:
            store_parts(e2, chunk)

    sum_copies = []

    def collect(chunk, which_layer, j):
        s = which_layer * SLOTS + j
        part = parts[chunk]
        return (
            part[0, inverse[0, s]].astype(F32)
            + part[1, inverse[1, s]].astype(F32)
            + part[2, inverse[2, s]].astype(F32)
        )

    for chunk in range(N_CHUNK):
        part_copies[2 * chunk].wait_recv()
        part_copies[2 * chunk + 1].wait_recv()
        for i, (which, device) in enumerate(((far_layer, across), (up_layer, up), (down_layer, down))):
            for j in range(SLOTS):
                sums[chunk][i, j] = collect(chunk, which, j).astype(BF16)
            index = 3 * chunk + i
            sum_copies.append(
                remote(sums[chunk].at[i], got[chunk].at[i], sum_send.at[index], sum_recv.at[index], device)
            )
            sum_copies[-1].start()

    for chunk, (energy, row, rows) in enumerate(CHUNKS):
        for i in range(3):
            sum_copies[3 * chunk + i].wait_recv()
        for j in range(SLOTS):
            outs[energy][j, pl.ds(row, rows)] = collect(chunk, layer, j) + (
                got[chunk][0, j].astype(F32) + got[chunk][1, j].astype(F32) + got[chunk][2, j].astype(F32)
            )

    for c in ids_copies + started + part_copies + sum_copies:
        c.wait_send()


def write_out(dens_ref, energy_ref, dens_out, energy_out, sems):
    copies = [
        pltpu.make_async_copy(dens_ref, dens_out, sems.at[0]),
        pltpu.make_async_copy(energy_ref, energy_out, sems.at[1]),
    ]
    for c in copies:
        c.start()
    for c in copies:
        c.wait()


def solution(mesh):
    n_slab = mesh.shape["slab"]

    def step(hamilton_blocks, pair_ids, weights, potential):
        hbm = pl.BlockSpec(memory_space=pltpu.HBM)
        vmem = pl.BlockSpec(memory_space=pltpu.VMEM)
        dma = pltpu.SemaphoreType.DMA
        out = jax.ShapeDtypeStruct((SLOTS, BS, BS), F32)
        sums = pl.pallas_call(
            functools.partial(kernel, n_slab),
            out_shape=(pltpu.VMEM(out.shape, F32), pltpu.VMEM(out.shape, F32)),
            in_specs=[hbm, hbm, hbm, pl.BlockSpec(memory_space=pltpu.SMEM)],
            out_specs=(vmem, vmem),
            scratch_shapes=[
                pltpu.VMEM((48, BS, BS), BF16),
                *[pltpu.VMEM((3, NPS + 1, rows, BS), BF16) for _, _, rows in CHUNKS],
                *[pltpu.VMEM((3, SLOTS, rows, BS), BF16) for _, _, rows in CHUNKS],
                *[pltpu.VMEM((3, SLOTS, rows, BS), BF16) for _, _, rows in CHUNKS],
                pltpu.SMEM((1, NPS), jnp.int32),
                pltpu.SMEM((1, NPS), F32),
                pltpu.SMEM((2, 1, NPS), jnp.int32),
                pltpu.SMEM((3, 16), jnp.int32),
                pltpu.VMEM((ORDER, ORDER), F32),
                pltpu.SemaphoreType.REGULAR,
                dma,
                dma((2,)),
                dma((20,)),
                dma((20,)),
                dma((2,)),
                dma((2,)),
                dma((2 * N_CHUNK,)),
                dma((2 * N_CHUNK,)),
                dma((3 * N_CHUNK,)),
                dma((3 * N_CHUNK,)),
            ],
            compiler_params=pltpu.CompilerParams(
                collective_id=0, has_side_effects=True, vmem_limit_bytes=48 * 1024 * 1024
            ),
        )(*[pltpu.with_memory_space_constraint(x, pltpu.HBM) for x in (hamilton_blocks, pair_ids, weights)], potential)
        return pl.pallas_call(
            write_out,
            out_shape=(pltpu.HBM(out.shape, F32), pltpu.HBM(out.shape, F32)),
            in_specs=[vmem, vmem],
            out_specs=(hbm, hbm),
            scratch_shapes=[dma((2,))],
        )(*[pltpu.with_memory_space_constraint(x, pltpu.VMEM) for x in sums])

    return jax.shard_map(
        step,
        mesh=mesh,
        in_specs=(P(("slab", "layer"), None, None), P(("slab", "layer"), None), P(("slab", "layer"), None), P()),
        out_specs=(P(("slab", "layer"), None, None), P(("slab", "layer"), None, None)),
        check_vma=False,
    )
```

```python
import functools

import jax
import jax.numpy as jnp
import numpy as np
from jax import lax
from jax.experimental import pallas as pl
from jax.experimental.pallas import tpu as pltpu
from jax.sharding import PartitionSpec as P

BS = 128
NB = 4
NPS = 10
ORDER = 512
SLOTS = 4
ROWS = 32
AFTER = 1
CHUNKS = tuple((energy, row, ROWS) for energy in range(2) for row in range(0, BS, ROWS))
N_CHUNK = len(CHUNKS)
MESH = pl.DeviceIdType.MESH
F32 = jnp.float32
BF16 = jnp.bfloat16
PAIRS = [(a, b) for a in range(NB) for b in range(a, NB)]
NO_PART = NPS


def mm(a, b):
    return jnp.dot(a, b, preferred_element_type=F32)


def eye(order, value):
    r = lax.broadcasted_iota(jnp.int32, (order, order), 0)
    c = lax.broadcasted_iota(jnp.int32, (order, order), 1)
    return jnp.where(r == c, value, 0.0)


def mean_square(m, n):
    total = jnp.zeros((BS, BS), F32)
    for a in range(NB):
        for b in range(NB):
            s, t = slice(a * BS, (a + 1) * BS), slice(b * BS, (b + 1) * BS)
            total += m[s, t] * n[s, t]
    return jnp.sum(total, keepdims=True) * (1.0 / ORDER)


def mean_diagonal(m):
    total = None
    for a in range(NB):
        s = slice(a * BS, (a + 1) * BS)
        r = lax.broadcasted_iota(jnp.int32, (BS, BS), 0)
        c = lax.broadcasted_iota(jnp.int32, (BS, BS), 1)
        part = jnp.where(r == c, m[s, s], 0.0)
        total = part if total is None else total + part
    return jnp.sum(total, keepdims=True) * (1.0 / ORDER)


def kernel(n_slab, hb_ref, ids_hbm, w_hbm, mu_ref, dens_ref, energy_ref, near, *rest):
    parts, sums, got = (rest[i * N_CHUNK : (i + 1) * N_CHUNK] for i in range(3))
    ids_ref, w_ref, remote_ids, inverse, h_mat, joined, local_sem, small_sem = rest[3 * N_CHUNK : 3 * N_CHUNK + 8]
    gather_send, gather_recv, ids_send, ids_recv, part_send, part_recv, sum_send, sum_recv = rest[3 * N_CHUNK + 8 :]
    outs = (dens_ref, energy_ref)
    slab = lax.axis_index("slab")
    layer = lax.axis_index("layer")
    core = lax.rem(slab, 2)
    partner_slab = slab + 1 - 2 * core
    other_slab = lax.rem(slab - 1 + 2 * core + n_slab, n_slab)
    up_layer = lax.rem(layer + 1, 4)
    down_layer = lax.rem(layer + 3, 4)
    far_layer = lax.rem(layer + 2, 4)
    up, down = (slab, up_layer), (slab, down_layer)
    partner, other, across = (partner_slab, layer), (other_slab, layer), (slab, far_layer)

    def remote(src, dst, send, recv, device):
        return pltpu.make_async_remote_copy(
            src_ref=src, dst_ref=dst, send_sem=send, recv_sem=recv, device_id=device, device_id_type=MESH
        )

    barrier = pltpu.get_barrier_semaphore()
    for device in (up, down, partner, across):
        pl.semaphore_signal(barrier, inc=1, device_id=device, device_id_type=MESH)

    @pl.when(core == 0)
    def _():
        pl.semaphore_signal(barrier, inc=1, device_id=other, device_id_type=MESH)

    locals_ = [pltpu.make_async_copy(hb_ref, near.at[pl.ds(layer * SLOTS, SLOTS)], local_sem)]
    for i, (src, dst) in enumerate(((ids_hbm, ids_ref), (w_hbm, w_ref))):
        locals_.append(pltpu.make_async_copy(src, dst, small_sem.at[i]))
    for c in locals_:
        c.start()
    for (_, _, rows), part in zip(CHUNKS, parts):
        for j in range(3):
            part[j, NO_PART] = jnp.zeros((rows, BS), BF16)
    pl.semaphore_wait(barrier, 4 + core)

    @pl.when(core == 1)
    def _():
        pl.semaphore_signal(joined, inc=1, device_id=other, device_id_type=MESH)


    def piece(group, which_layer, first, count):
        return near.at[pl.ds(group * 16 + which_layer * SLOTS + first, count)]

    started = []

    def send(src, group, which_layer, first, count, index, device):
        c = remote(src, piece(group, which_layer, first, count), gather_send.at[index], gather_recv.at[index], device)
        c.start()
        started.append(c)

    def wait_recv(group, which_layer, first, count, index):
        at = piece(group, which_layer, first, count)
        remote(at, at, gather_send.at[index], gather_recv.at[index], up).wait_recv()

    locals_[0].wait()
    send(piece(0, layer, 0, 2), 0, layer, 0, 2, 0, up)
    send(piece(0, layer, 2, 2), 0, layer, 2, 2, 1, down)
    own_to_other = remote(
        piece(0, layer, 0, 4), piece(2, layer, 0, 4), gather_send.at[2], gather_recv.at[2], other
    )
    started.append(own_to_other)

    @pl.when(core == 1)
    def _():
        own_to_other.start()

    send(piece(0, layer, 2, 2), 0, layer, 2, 2, 3, up)
    send(piece(0, layer, 0, 2), 0, layer, 0, 2, 4, down)
    send(piece(0, layer, 0, 4), 1, layer, 0, 4, 5, partner)
    send(piece(0, layer, 0, 2), 0, layer, 0, 2, 6, across)
    send(piece(0, layer, 2, 2), 0, layer, 2, 2, 7, across)
    ids_copies = [
        remote(ids_hbm, remote_ids.at[j], ids_send.at[j], ids_recv.at[j], device)
        for j, device in enumerate((partner, other))
    ]
    ids_copies[0].start()

    relays = (
        (down_layer, 0, 0),
        (up_layer, 2, 1),
        (down_layer, 2, 3),
        (up_layer, 0, 4),
        (far_layer, 0, 6),
        (far_layer, 2, 7),
    )
    for i, (which, first, index) in enumerate(relays):
        wait_recv(0, which, first, 2, index)
        send(piece(0, which, first, 2), 1, which, first, 2, 14 + i, partner)
        if i == AFTER:

            @pl.when(core == 0)
            def _():
                pl.semaphore_wait(joined, 1)
                own_to_other.start()

            ids_copies[1].start()
        for k in range(i + 1) if i == AFTER else [i] if i > AFTER else []:
            send(piece(0, relays[k][0], relays[k][1], 2), 2, relays[k][0], relays[k][1], 2, 8 + k, other)

    for c in locals_[1:]:
        c.wait()
    for c in ids_copies:
        c.wait_recv()

    def find(s, _):
        want = slab * 16 + s
        found = [NO_PART + 0 * want for _ in range(3)]
        for k in range(NPS):
            found[0] = jnp.where(ids_ref[0, k] == want, k, found[0])
            found[1] = jnp.where(remote_ids[0, 0, k] == want, k, found[1])
            found[2] = jnp.where(remote_ids[1, 0, k] == want, k, found[2])
        for j in range(3):
            inverse[j, s] = found[j]
        return 0

    lax.fori_loop(0, 16, find, 0)

    wait_recv(1, layer, 0, 4, 5)
    wait_recv(2, layer, 0, 4, 2)
    for i, (which, first, _) in enumerate(relays):
        wait_recv(1, which, first, 2, 14 + i)
        wait_recv(2, which, first, 2, 8 + i)

    for k, (a, b) in enumerate(PAIRS):
        request = ids_ref[0, k]
        its_slab = request // 16
        group = jnp.where(its_slab == slab, 0, jnp.where(its_slab == partner_slab, 1, 2))
        block = near[group * 16 + request - its_slab * 16]
        ra, rb = pl.ds(a * BS, BS), pl.ds(b * BS, BS)
        if a == b:
            h_mat[ra, ra] = block.astype(F32) + block.T.astype(F32)
        else:
            h_mat[ra, rb] = block.astype(F32)
            h_mat[rb, ra] = block.T.astype(F32)
    h = h_mat[...]
    mu = mu_ref[0]
    norm2 = jnp.zeros((BS, BS), F32)
    for a in range(NB):
        for b in range(NB):
            block = h[a * BS : (a + 1) * BS, b * BS : (b + 1) * BS]
            if a == b:
                block = eye(BS, mu) - block
            norm2 += block * block
    norm2 = jnp.sum(norm2, keepdims=True) * (1.0 / ORDER) + 1e-06
    inv = 0.5 * lax.rsqrt(norm2)
    hb = h.astype(BF16)
    x0 = mu * inv
    s0 = (inv * inv) * mm(hb, hb) - (2.0 * x0 * inv) * h + eye(ORDER, x0 * x0 - 0.25)
    x1 = (-1.375 * inv) * h - (0.5 * x0) * s0 + (0.5 * inv) * mm(hb, s0.astype(BF16)) + eye(ORDER, 1.375 * x0)
    t1 = 1.375 * (x0 - inv * mean_diagonal(h)) - (0.5 * x0) * mean_diagonal(s0) + (0.5 * inv) * mean_square(h, s0)
    b1 = x1 - eye(ORDER, t1)
    b1h = b1.astype(BF16)
    u0 = mean_square(b1, b1)
    s1 = mm(b1h, b1h) + (2.0 * t1) * b1 - eye(ORDER, u0)
    u1 = u0 + t1 * t1
    s1h = s1.astype(BF16)

    def rows_of(m, row, rows):
        return jnp.concatenate([m[a * BS + row : a * BS + row + rows] for a in range(NB)], axis=0)

    weights = [0.5 * w_ref[0, k] for k in range(NPS)]
    part_copies = []

    def store_parts(matrix, chunk):
        energy, row, rows = CHUNKS[chunk]
        for k, (a, b) in enumerate(PAIRS):
            first = a * BS + row if energy else a * rows
            block = matrix[first : first + rows, b * BS : (b + 1) * BS]
            if not energy and a == b:
                r = lax.broadcasted_iota(jnp.int32, (rows, BS), 0) + row
                c = lax.broadcasted_iota(jnp.int32, (rows, BS), 1)
                block = block + jnp.where(r == c, 1.0, 0.0)
            parts[chunk][0, k] = (weights[k] * block).astype(BF16)
        for j, device in ((2, other), (1, partner)):
            c = remote(
                parts[chunk].at[0, pl.ds(0, NPS)],
                parts[chunk].at[j, pl.ds(0, NPS)],
                part_send.at[2 * chunk + j - 1],
                part_recv.at[2 * chunk + j - 1],
                device,
            )
            c.start()
            part_copies.append(c)

    strips = []
    for chunk, (energy, row, rows) in enumerate(CHUNKS):
        if not energy:
            strip = (1.5 - 0.5 * u1) * rows_of(x1, row, rows) - (0.5 * t1) * rows_of(s1, row, rows)
            strip = strip - 0.5 * mm(rows_of(b1h, row, rows), s1h)
            store_parts(strip, chunk)
            strips.append((rows, strip))
    x2 = jnp.concatenate([m[a * r : (a + 1) * r] for a in range(NB) for r, m in strips], axis=0)

    t2 = mean_diagonal(x2)
    c2 = x2 - eye(ORDER, t2)
    c2h = c2.astype(BF16)
    c2l = (c2 - c2h.astype(F32)).astype(BF16)
    hl = (h - hb.astype(F32)).astype(BF16)
    e2 = (1.0 + t2) * h + mm(c2h, hb) + mm(c2l, hb) + mm(c2h, hl)
    for chunk in range(N_CHUNK):
        if CHUNKS[chunk][0]:
            store_parts(e2, chunk)

    sum_copies = []

    def collect(chunk, which_layer, j):
        s = which_layer * SLOTS + j
        part = parts[chunk]
        return (
            part[0, inverse[0, s]].astype(F32)
            + part[1, inverse[1, s]].astype(F32)
            + part[2, inverse[2, s]].astype(F32)
        )

    for chunk in range(N_CHUNK):
        part_copies[2 * chunk].wait_recv()
        part_copies[2 * chunk + 1].wait_recv()
        for i, (which, device) in enumerate(((far_layer, across), (up_layer, up), (down_layer, down))):
            for j in range(SLOTS):
                sums[chunk][i, j] = collect(chunk, which, j).astype(BF16)
            index = 3 * chunk + i
            sum_copies.append(
                remote(sums[chunk].at[i], got[chunk].at[i], sum_send.at[index], sum_recv.at[index], device)
            )
            sum_copies[-1].start()

    for chunk, (energy, row, rows) in enumerate(CHUNKS):
        for i in range(3):
            sum_copies[3 * chunk + i].wait_recv()
        for j in range(SLOTS):
            outs[energy][j, pl.ds(row, rows)] = collect(chunk, layer, j) + (
                got[chunk][0, j].astype(F32) + got[chunk][1, j].astype(F32) + got[chunk][2, j].astype(F32)
            )

    for c in ids_copies + started + part_copies + sum_copies:
        c.wait_send()


def write_out(dens_ref, energy_ref, dens_out, energy_out, sems):
    copies = [
        pltpu.make_async_copy(dens_ref, dens_out, sems.at[0]),
        pltpu.make_async_copy(energy_ref, energy_out, sems.at[1]),
    ]
    for c in copies:
        c.start()
    for c in copies:
        c.wait()


def solution(mesh):
    n_slab = mesh.shape["slab"]

    def step(hamilton_blocks, pair_ids, weights, potential):
        hbm = pl.BlockSpec(memory_space=pltpu.HBM)
        vmem = pl.BlockSpec(memory_space=pltpu.VMEM)
        dma = pltpu.SemaphoreType.DMA
        out = jax.ShapeDtypeStruct((SLOTS, BS, BS), F32)
        sums = pl.pallas_call(
            functools.partial(kernel, n_slab),
            out_shape=(pltpu.VMEM(out.shape, F32), pltpu.VMEM(out.shape, F32)),
            in_specs=[hbm, hbm, hbm, pl.BlockSpec(memory_space=pltpu.SMEM)],
            out_specs=(vmem, vmem),
            scratch_shapes=[
                pltpu.VMEM((48, BS, BS), BF16),
                *[pltpu.VMEM((3, NPS + 1, rows, BS), BF16) for _, _, rows in CHUNKS],
                *[pltpu.VMEM((3, SLOTS, rows, BS), BF16) for _, _, rows in CHUNKS],
                *[pltpu.VMEM((3, SLOTS, rows, BS), BF16) for _, _, rows in CHUNKS],
                pltpu.SMEM((1, NPS), jnp.int32),
                pltpu.SMEM((1, NPS), F32),
                pltpu.SMEM((2, 1, NPS), jnp.int32),
                pltpu.SMEM((3, 16), jnp.int32),
                pltpu.VMEM((ORDER, ORDER), F32),
                pltpu.SemaphoreType.REGULAR,
                dma,
                dma((2,)),
                dma((20,)),
                dma((20,)),
                dma((2,)),
                dma((2,)),
                dma((2 * N_CHUNK,)),
                dma((2 * N_CHUNK,)),
                dma((3 * N_CHUNK,)),
                dma((3 * N_CHUNK,)),
            ],
            compiler_params=pltpu.CompilerParams(
                collective_id=0, has_side_effects=True, vmem_limit_bytes=48 * 1024 * 1024
            ),
        )(*[pltpu.with_memory_space_constraint(x, pltpu.HBM) for x in (hamilton_blocks, pair_ids, weights)], potential)
        return pl.pallas_call(
            write_out,
            out_shape=(pltpu.HBM(out.shape, F32), pltpu.HBM(out.shape, F32)),
            in_specs=[vmem, vmem],
            out_specs=(hbm, hbm),
            scratch_shapes=[dma((2,))],
        )(*[pltpu.with_memory_space_constraint(x, pltpu.VMEM) for x in sums])

    return jax.shard_map(
        step,
        mesh=mesh,
        in_specs=(P(("slab", "layer"), None, None), P(("slab", "layer"), None), P(("slab", "layer"), None), P()),
        out_specs=(P(("slab", "layer"), None, None), P(("slab", "layer"), None, None)),
        check_vma=False,
    )
```
